32 devices in a mesh: gx: 4 (over x, core), gy: 8 (over z, y).
Axes of the slice: x: 2, y: 2, z: 4, core: 2. Of those that a mesh axis runs over, the one named last changes fastest.
Arguments:
- velocity: float32 [3, 1024, 512], P(None, ('gx', 'gy')), may hold values from -6 to 6
- depart: float32 [3, 524288], P(None, ('gx', 'gy')), may hold values from -1 to 1
- owner_rank: int32 [524288, 1], P(('gx', 'gy')), may hold values from 0 to 31; in each aligned block of 16384 rows (0 to 16383, 16384 to 32767, ...) at most 1024 rows name the same one
- owner_element_index: int32 [524288], P(('gx', 'gy')), may hold values from 0 to 31
- neighbours: int32 [6, 1024], P(None, ('gx', 'gy')), may hold values from -1 to 1023, as said below
Outputs:
- advected: float32 [3, 1024, 512], P(None, ('gx', 'gy'))
The draws below stay inside these ranges and needn't reach their ends.
Inputs may be any that keep to these rules, and one draw needn't show every extreme that they name: `owner_rank`: within the rows of one device no owner device is named by more than 1024 rows, and in some device's rows one owner is named exactly 1024 times. `neighbours`: -1 marks a boundary face; any other entry is an element of the same block of 32 consecutive elements as the entry's own element, or of the block just before or just after it.
All inputs are finite; a program needn't handle non-finite values.
Results may differ from the reference program's by a relative error of at most 0.0003.
Values sent between devices are 32-bit elements; how exact they have to be, the bound alone decides.
A program may use at most 64 MiB of HBM per device.

```python
import math
import jax
import jax.numpy as jnp
import numpy as np
from jax import lax

VELOCITY_PARTS = 3
NODES = 512
E_DEV = 32
ELEMS = 1024
POINTS = 524288
CAP = 1024
DEVICES = 32


def draw_neighbours(key, part):
    elem_total = ELEMS
    element = jnp.arange(elem_total, dtype=jnp.int32)
    block_of = element // E_DEV
    lowest = jnp.maximum(block_of - 1, 0) * E_DEV
    highest = jnp.minimum(block_of + 2, elem_total // E_DEV) * E_DEV
    pick_key, edge_key = jax.random.split(key)
    offset = jax.random.randint(pick_key, (6, elem_total), 0, 1 << 30, dtype=jnp.int32) % (highest - lowest)[None, :]
    picked = lowest[None, :] + offset
    boundary = jax.random.randint(edge_key, (6, elem_total), 0, 6, dtype=jnp.int32)
    return jnp.where(boundary == 0, -1, picked).astype(jnp.int32)


def place_ends(drawn, rng, least, high):
    spot = [jax.random.randint(jax.random.fold_in(rng, axis), (), 0, length) for axis, length in enumerate(drawn.shape)]
    widest = drawn.shape.index(max(drawn.shape))
    beside = spot[:widest] + [(spot[widest] + 1) % drawn.shape[widest]] + spot[widest + 1:]
    return drawn.at[tuple(spot)].set(least).at[tuple(beside)].set(high)


def shard_levels(rng, shape, shards, smallest, largest):
    level = 1.0
    for axis_at, parts in shards:
        steps = jax.random.uniform(jax.random.fold_in(jax.random.fold_in(rng, 6), axis_at), (parts,), jnp.float32, smallest / len(shards), largest / len(shards))
        level = level * jnp.repeat(jnp.exp(steps), shape[axis_at] // parts).reshape((-1,) + (1,) * (len(shape) - 1 - axis_at))
    return level


def shared_out(rng, own, number, rows, number_of, top, reach, skew):
    ranking = jax.random.permutation(rng, number_of)
    crowded, ordinary = portions_of(number_of, rows * top, reach, skew, True), portions_of(number_of, rows * top, reach, skew, False)
    places = jnp.arange(number_of)

    def named(lengths, turn):
        used = int((lengths > 0).sum())
        fixed = max(1, used // 4)
        moved = fixed + (places - fixed + turn * (used - fixed)) % max(1, number_of - fixed)
        return jnp.zeros((number_of,), jnp.int32).at[ranking[jnp.where(places < fixed, places, moved)]].set(jnp.asarray(lengths, jnp.int32))

    lengths = jnp.where(number % 4 == 0, named(crowded, number // 4), named(ordinary, number - number // 4 - 1))
    mixed = jax.random.permutation(jax.random.fold_in(own, 3), number_of)
    source_of, receiver = mixed[0:number_of // 2 * 2:2], mixed[1:number_of // 2 * 2:2]
    room = jnp.minimum(lengths[source_of] - 1, reach - lengths[receiver]) // 2
    room = jnp.where((source_of == ranking[0]) | (receiver == ranking[0]) | (lengths[receiver] == 0), 0, jnp.maximum(room, 0))
    moved = jax.random.randint(jax.random.fold_in(own, 4), (number_of // 2,), 0, 1 << 20) % (room + 1)
    lengths = lengths.at[source_of].add(-moved).at[receiver].add(moved)
    members = jnp.searchsorted(jnp.cumsum(lengths), jnp.arange(rows * top), side="right").astype(jnp.int32)
    listing = members.reshape(top, rows).T
    listing = listing[jax.random.permutation(jax.random.fold_in(own, 1), rows)]
    turn = jax.random.randint(jax.random.fold_in(own, 2), (rows, 1), 0, top)
    return jnp.take_along_axis(listing, (jnp.arange(top)[None, :] + turn) % top, axis=1)


def portions_of(amount, total, most, lean, full):
    weights = [(1 << 20) // math.isqrt(standing ** lean) + 1 for standing in range(1, amount + 1)]
    largest = most if full else min(most, max(-(-total // amount), total * weights[0] // sum(weights)))
    least = 1 if total - largest >= amount - 1 else 0
    counts, surplus = [largest] + [least] * (amount - 1), total - largest - least * (amount - 1)
    while surplus > 0:
        candidates = [i for i in range(1, amount) if counts[i] < largest] or [i for i in range(1, amount) if counts[i] < most]
        whole, left = sum([weights[i] for i in candidates]), surplus
        for i in candidates:
            extra = min(most - counts[i], max(1, left * weights[i] // whole), surplus)
            counts[i] = counts[i] + extra
            surplus = surplus - extra
    return np.array(counts)


def gaussian(stream_key, extent, scale, limit, cuts=(), kind=jnp.bfloat16):
    values = jax.random.normal(stream_key, extent, jnp.float32) * scale
    if len(cuts) > 0:
        values = shard_levels(stream_key, extent, cuts, -0.22, 0.18) * values
    return jnp.clip(values, min=-limit, max=limit).astype(kind)


def setup_inputs(seed: int = 0) -> dict:
    splits = jax.random.split(jax.random.key(seed), 6)
    velocity = gaussian(splits[0], (VELOCITY_PARTS, ELEMS, NODES), 1.0, 6.0, ((1, 32),), jnp.float32)
    depart = jnp.clip(jax.random.uniform(splits[1], (VELOCITY_PARTS, POINTS), jnp.float32, -1.0, 1.0) * shard_levels(splits[1], (VELOCITY_PARTS, POINTS), ((1, 32),), -0.4, 0.0), -1.0, 1.0)
    owner_rank_keys = jax.random.split(jax.random.fold_in(splits[2], 1), POINTS // (E_DEV * NODES))
    owner_rank_turns = jax.random.permutation(jax.random.fold_in(splits[2], 3), POINTS // (E_DEV * NODES))
    owner_rank = jax.vmap(lambda own, number: shared_out(jax.random.fold_in(splits[2], 2), own, number, E_DEV * NODES, DEVICES, 1, CAP, 2))(owner_rank_keys, owner_rank_turns).reshape((POINTS, 1))
    owner_element_index = place_ends(jax.random.randint(splits[3], (POINTS,), 0, E_DEV), jax.random.fold_in(splits[3], 1), 0, E_DEV - 1).astype(jnp.int32)
    neighbours = draw_neighbours(jax.random.fold_in(splits[5], 71), 0)
    return {"velocity": velocity, "depart": depart, "owner_rank": owner_rank, "owner_element_index": owner_element_index, "neighbours": neighbours}


GLL_POINTS = np.array([-1.0, -0.8717401485096066, -0.5917001814331423, -0.2092992179024789, 0.2092992179024789, 0.5917001814331423, 0.8717401485096066, 1.0])


def lagrange(coords):
    columns = []
    for node_id in range(8):
        factor = jnp.ones_like(coords)
        for other in range(8):
            if other != node_id:
                factor = factor * ((coords - float(GLL_POINTS[other])) / float(GLL_POINTS[node_id] - GLL_POINTS[other]))
        columns.append(factor)
    return jnp.stack(columns, axis=-1)


def face_slicer(face_id):
    whole_range = slice(None)
    edge_at = 7 * (face_id % 2)
    if face_id < 2:
        return (whole_range, whole_range, edge_at)
    if face_id < 4:
        return (whole_range, whole_range, whole_range, edge_at)
    return (whole_range, whole_range, whole_range, whole_range, edge_at)


def faces_of(nodal_cube):
    shape_lead = (nodal_cube.shape[0], nodal_cube.shape[1], 64)
    return jnp.stack([nodal_cube[face_slicer(face_id)].reshape(shape_lead) for face_id in range(6)], axis=1)


def apply_faces(nodal_cube, own_faces, neighbour_faces, local_index, present):
    result = nodal_cube
    for face_id in range(6):
        across_elements = neighbour_faces[:, face_id ^ 1][:, local_index[face_id]]
        change = jnp.where(present[face_id][None, :, None], 0.5 * (across_elements - own_faces[:, face_id]), 0.0)
        result = result.at[face_slicer(face_id)].add(change.reshape(result.shape[0], result.shape[1], 8, 8))
    return result


def reference(velocity, depart, owner_rank, owner_element_index, neighbours):
    owners = (owner_rank[:, 0] * E_DEV + owner_element_index).astype(jnp.int32)
    block_count = POINTS // 4096
    coord_blocks = depart.reshape(3, block_count, 4096).transpose(1, 0, 2)
    owner_blocks = owners.reshape(block_count, 4096)

    def one_block(block_pair):
        coords, owner_row_table = block_pair
        weights = lagrange(coords)
        gathered = jnp.take(velocity, owner_row_table, axis=1).reshape(3, 4096, 8, 8, 8)
        along = jnp.einsum("cbijk,bk->cbij", gathered, weights[2], precision=lax.Precision.HIGHEST)
        rs_plane = weights[0][:, :, None] * weights[1][:, None, :]
        return jnp.sum(along * rs_plane[None], axis=(2, 3))

    departed = lax.map(one_block, (coord_blocks, owner_blocks)).transpose(1, 0, 2)
    nodal_cube = departed.reshape(3, ELEMS, 8, 8, 8)
    own_faces = faces_of(nodal_cube)
    present = neighbours >= 0
    local_index = jnp.maximum(neighbours, 0).astype(jnp.int32)
    result = apply_faces(nodal_cube, own_faces, own_faces, local_index, present)
    return result.reshape(3, ELEMS, 512)
```

```python
import functools
import math

import jax
import jax.numpy as jnp
import numpy as np
from jax import lax
from jax.experimental import pallas as pl
from jax.experimental.pallas import tpu as pltpu
from jax.sharding import PartitionSpec as P

GLL_POINTS = np.array(
    [
        -1.0,
        -0.8717401485096066,
        -0.5917001814331423,
        -0.2092992179024789,
        0.2092992179024789,
        0.5917001814331423,
        0.8717401485096066,
        1.0,
    ]
)
F32, BF16 = jnp.float32, jnp.bfloat16


def lagrange_constants():
    table = np.zeros((8, 128))
    for i in range(8):
        table[i, 0] = 1.0 / np.prod([GLL_POINTS[i] - GLL_POINTS[m] for m in range(8) if m != i])
        for r in range(1, 8):
            table[i, r] = GLL_POINTS[(i + r) % 8]
    return table.astype(np.float32)


def face_selector():
    cube = np.arange(512).reshape(8, 8, 8)
    faces = [cube[0], cube[7], cube[:, 0], cube[:, 7], cube[:, :, 0], cube[:, :, 7]]
    nodes = np.concatenate([face.reshape(-1) for face in faces])
    return (np.arange(512)[:, None] == nodes[None, :]).astype(np.float32)


def split2(x):
    hi = x.astype(BF16).astype(F32)
    return hi, x - hi


def dot(a, b):
    return lax.dot_general(a, b, (((1,), (0,)), ((), ())), preferred_element_type=F32)


def dot_nt(a, b):
    return lax.dot_general(a, b, (((1,), (1,)), ((), ())), preferred_element_type=F32)


def place_kernel(peers, capacity, sub, owner_ref, coords_ref, elem_ref, upper_ref, send_ref, slot_ref, acc, carry):
    step = pl.program_id(0)

    @pl.when(step == 0)
    def _():
        acc[...] = jnp.zeros_like(acc)
        carry[...] = jnp.zeros_like(carry)

    block = owner_ref.shape[1]
    upper = upper_ref[...]
    peer_rows = lax.broadcasted_iota(jnp.int32, (peers, sub), 0)
    slots = []
    running = carry[:, 0:1]
    for part in range(block // sub):
        owner = owner_ref[:, part * sub : (part + 1) * sub]
        match = peer_rows == owner
        hot = match.astype(F32)
        earlier = dot(hot.astype(BF16), upper) + running
        slots.append(jnp.sum(jnp.where(match, earlier, 0.0), axis=0, keepdims=True))
        running = running + jnp.sum(hot, axis=1, keepdims=True)
    carry[...] = jnp.broadcast_to(running, carry.shape)
    slot = jnp.concatenate(slots, axis=1).astype(jnp.int32)
    slot_ref[...] = slot
    owner = jnp.broadcast_to(owner_ref[...], (8, block))
    hi, lo = split2(coords_ref[...])
    values = jnp.concatenate([hi, elem_ref[...].astype(F32), lo, jnp.zeros((1, block), F32)], axis=0)
    spread = jnp.concatenate([jnp.where(owner == p, values, 0.0) for p in range(peers)], axis=0).astype(BF16)
    for at in range(0, capacity, 256):
        width = min(256, capacity - at)
        rows = lax.broadcasted_iota(jnp.int32, (width, block), 0) + at
        hot = (rows == slot).astype(F32).astype(BF16)
        acc[:, at : at + width] += dot_nt(spread, hot)

    @pl.when(step == pl.num_programs(0) - 1)
    def _():
        for p in range(peers):
            both = acc[8 * p : 8 * p + 8]
            send_ref[p] = jnp.concatenate([both[0:3] + both[4:7], both[3:4]], axis=0)


def place(owner, coords, elem, peers, capacity):
    points = owner.shape[1]
    block, sub = math.gcd(points, 1024), math.gcd(points, 256)
    upper = np.triu(np.ones((sub, sub), np.float32), 1)
    return pl.pallas_call(
        functools.partial(place_kernel, peers, capacity, sub),
        grid=(points // block,),
        in_specs=[
            pl.BlockSpec((1, block), lambda i: (0, i)),
            pl.BlockSpec((3, block), lambda i: (0, i)),
            pl.BlockSpec((1, block), lambda i: (0, i)),
            pl.BlockSpec((sub, sub), lambda i: (0, 0)),
        ],
        out_specs=[
            pl.BlockSpec((peers, 4, capacity), lambda i: (0, 0, 0)),
            pl.BlockSpec((1, block), lambda i: (0, i)),
        ],
        out_shape=[
            jax.ShapeDtypeStruct((peers, 4, capacity), F32),
            jax.ShapeDtypeStruct((1, points), jnp.int32),
        ],
        scratch_shapes=[pltpu.VMEM((8 * peers, capacity), F32), pltpu.VMEM((peers, 128), F32)],
        compiler_params=pltpu.CompilerParams(dimension_semantics=("arbitrary",)),
        name="place",
    )(owner, coords, elem, jnp.asarray(upper, BF16))


def interp_kernel(elems, chunk, points_ref, table_ref, const_ref, out_ref, stacked):
    @pl.when(pl.program_id(0) == 0)
    def _():
        hi, lo = split2(table_ref[...])
        stacked[...] = jnp.concatenate([hi, hi, lo], axis=1).astype(BF16)

    slots = points_ref.shape[2]
    for at in range(0, slots, chunk):
        x = points_ref[0, :, at : at + chunk]
        weights = []
        for d in range(3):
            coord = jnp.broadcast_to(x[d : d + 1], (8, chunk))
            w = const_ref[:, 0:1] * (coord - const_ref[:, 1:2])
            for r in range(2, 8):
                w = w * (coord - const_ref[:, r : r + 1])
            weights.append(w)
        elem = jnp.broadcast_to(x[3:4], (8, chunk))
        hi, lo = split2(weights[2])
        picks = [elem == float(e) for e in range(elems)]
        a_hi = jnp.concatenate([jnp.where(pick, hi, 0.0) for pick in picks], axis=0).astype(BF16)
        a_lo = jnp.concatenate([jnp.where(pick, lo, 0.0) for pick in picks], axis=0).astype(BF16)
        summed = dot(stacked[...], jnp.concatenate([a_hi, a_lo, a_hi], axis=0))
        results = []
        for c in range(3):
            total = None
            for i in range(8):
                term = summed[64 * c + 8 * i : 64 * c + 8 * i + 8] * weights[0][i : i + 1]
                total = term if total is None else total + term
            results.append(jnp.sum(total * weights[1], axis=0, keepdims=True))
        out_ref[0, :, at : at + chunk] = jnp.concatenate(results, axis=0)


def interpolate(points, table):
    peers, _, slots = points.shape
    elems = table.shape[1] // 8
    chunk = math.gcd(slots, 256)
    return pl.pallas_call(
        functools.partial(interp_kernel, elems, chunk),
        grid=(peers,),
        in_specs=[
            pl.BlockSpec((1, 4, slots), lambda i: (i, 0, 0)),
            pl.BlockSpec(table.shape, lambda i: (0, 0)),
            pl.BlockSpec((8, 128), lambda i: (0, 0)),
        ],
        out_specs=pl.BlockSpec((1, 3, slots), lambda i: (i, 0, 0)),
        out_shape=jax.ShapeDtypeStruct((peers, 3, slots), F32),
        scratch_shapes=[pltpu.VMEM((192, 3 * table.shape[1]), BF16)],
        compiler_params=pltpu.CompilerParams(dimension_semantics=("arbitrary",)),
        name="interp",
    )(points, table, jnp.asarray(lagrange_constants()))


def pick_kernel(peers, per_step, answers_ref, owner_ref, slot_ref, select_ref, out_ref, faces_ref, halves):
    step = pl.program_id(0)
    capacity = answers_ref.shape[2]

    @pl.when(step == 0)
    def _():
        gap = jnp.zeros((1, capacity), F32)
        for p in range(0, peers, 2):
            rows = []
            for q in (p, p + 1):
                hi, lo = split2(answers_ref[q])
                rows += [hi, gap, lo, gap]
            halves[8 * p : 8 * p + 16] = jnp.concatenate(rows, axis=0).astype(BF16)

    for at in range(per_step):
        nodes = slice(512 * at, 512 * at + 512)
        slot = slot_ref[:, nodes]
        rows = lax.broadcasted_iota(jnp.int32, (capacity, 512), 0)
        hot = (rows == slot).astype(F32).astype(BF16)
        picked = dot(halves[...], hot)
        owner = jnp.broadcast_to(owner_ref[:, nodes], (8, 512))
        total = jnp.zeros((8, 512), F32)
        for p in range(peers):
            total = total + jnp.where(owner == p, picked[8 * p : 8 * p + 8], 0.0)
        for c in range(3):
            out_ref[c, pl.ds(step * per_step + at, 1), :] = total[c : c + 1] + total[c + 4 : c + 5]

    @pl.when(step == pl.num_programs(0) - 1)
    def _():
        for c in range(3):
            hi, lo = split2(out_ref[c])
            mid, low = split2(lo)
            sel = select_ref[...]
            faces_ref[c] = dot(hi.astype(BF16), sel) + dot(mid.astype(BF16), sel) + dot(low.astype(BF16), sel)


def pick(answers, owner, slot, elems, select):
    peers, _, capacity = answers.shape
    points = owner.shape[1]
    per_step = math.gcd(elems, 2)
    block = per_step * 512
    return pl.pallas_call(
        functools.partial(pick_kernel, peers, per_step),
        grid=(points // block,),
        in_specs=[
            pl.BlockSpec(answers.shape, lambda i: (0, 0, 0)),
            pl.BlockSpec((1, block), lambda i: (0, i)),
            pl.BlockSpec((1, block), lambda i: (0, i)),
            pl.BlockSpec((512, 384), lambda i: (0, 0)),
        ],
        out_specs=[
            pl.BlockSpec((3, elems, 512), lambda i: (0, 0, 0)),
            pl.BlockSpec((3, elems, 384), lambda i: (0, 0, 0)),
        ],
        out_shape=[
            jax.ShapeDtypeStruct((3, elems, 512), F32),
            jax.ShapeDtypeStruct((3, elems, 384), F32),
        ],
        scratch_shapes=[pltpu.VMEM((8 * peers, capacity), BF16)],
        compiler_params=pltpu.CompilerParams(dimension_semantics=("arbitrary",)),
        name="pick",
    )(answers, owner, slot, select)


def faces_kernel(interp_ref, own_ref, prev_ref, next_ref, index_ref, select_ref, out_ref):
    elems = interp_ref.shape[1]
    index = index_ref[...]
    columns = lax.broadcasted_iota(jnp.int32, (6 * elems, 3 * elems), 1)
    picker = (columns == index).astype(F32).astype(BF16)
    present = (index >= 0).astype(F32)
    for c in range(3):
        own = own_ref[c]
        extended = jnp.concatenate([prev_ref[c], own, next_ref[c]], axis=0)
        hi, lo = split2(extended)
        across = dot(picker, hi.astype(BF16)) + dot(picker, lo.astype(BF16))
        changes = []
        for f in range(6):
            g = f ^ 1
            rows = slice(f * elems, (f + 1) * elems)
            other = across[rows, 64 * g : 64 * g + 64]
            changes.append(0.5 * (other - present[rows] * own[:, 64 * f : 64 * f + 64]))
        hi, lo = split2(jnp.concatenate(changes, axis=1))
        sel = select_ref[...]
        out_ref[c] = interp_ref[c] + dot_nt(hi.astype(BF16), sel) + dot_nt(lo.astype(BF16), sel)


def local(velocity, depart, owner_rank, owner_element_index, neighbours):
    axes = ("gx", "gy")
    inner_count = lax.axis_size("gy")
    peers = lax.axis_size("gx") * inner_count
    elems = velocity.shape[1]
    points = depart.shape[1]
    capacity = 2 * points // peers
    owner = owner_rank.reshape(1, points)
    select = jnp.asarray(face_selector(), BF16)
    send, slot = place(owner, depart, owner_element_index.reshape(1, points), peers, capacity)
    received = lax.all_to_all(send, axes, split_axis=0, concat_axis=0, tiled=True)
    table = velocity.reshape(3, elems, 64, 8).transpose(0, 2, 1, 3).reshape(192, elems * 8)
    answers = interpolate(received, table)
    answers = lax.all_to_all(answers, axes, split_axis=0, concat_axis=0, tiled=True)
    interp, faces = pick(answers, owner, slot, elems, select)
    before = lax.ppermute(faces, axes, [(i, i + 1) for i in range(peers - 1)])
    after = lax.ppermute(faces, axes, [(i + 1, i) for i in range(peers - 1)])
    device_id = lax.axis_index("gx") * inner_count + lax.axis_index("gy")
    index = jnp.where(neighbours >= 0, neighbours - (device_id - 1) * elems, -1)
    return pl.pallas_call(
        faces_kernel,
        out_shape=jax.ShapeDtypeStruct((3, elems, 512), F32),
        name="faces",
    )(interp, faces, before, after, index.reshape(6 * elems, 1), select)


def solution(mesh):
    placed = (
        P(None, ("gx", "gy"), None),
        P(None, ("gx", "gy")),
        P(("gx", "gy"), None),
        P(("gx", "gy")),
        P(None, ("gx", "gy")),
    )
    return jax.shard_map(
        local, mesh=mesh, in_specs=placed, out_specs=P(None, ("gx", "gy"), None), check_vma=False
    )
```

```python
import functools
import math

import jax
import jax.numpy as jnp
import numpy as np
from jax import lax
from jax.experimental import pallas as pl
from jax.experimental.pallas import tpu as pltpu
from jax.sharding import PartitionSpec as P

GLL_POINTS = np.array(
    [
        -1.0,
        -0.8717401485096066,
        -0.5917001814331423,
        -0.2092992179024789,
        0.2092992179024789,
        0.5917001814331423,
        0.8717401485096066,
        1.0,
    ]
)
F32, BF16 = jnp.float32, jnp.bfloat16
MESH = pl.DeviceIdType.MESH


def lagrange_constants():
    table = np.zeros((8, 128))
    for i in range(8):
        table[i, 0] = 1.0 / np.prod([GLL_POINTS[i] - GLL_POINTS[m] for m in range(8) if m != i])
        for r in range(1, 8):
            table[i, r] = GLL_POINTS[(i + r) % 8]
    return table.astype(np.float32)


def face_selector():
    cube = np.arange(512).reshape(8, 8, 8)
    faces = [cube[0], cube[7], cube[:, 0], cube[:, 7], cube[:, :, 0], cube[:, :, 7]]
    nodes = np.concatenate([face.reshape(-1) for face in faces])
    return (np.arange(512)[:, None] == nodes[None, :]).astype(np.float32)


def split2(x):
    hi = x.astype(BF16).astype(F32)
    return hi, x - hi


def dot(a, b):
    return lax.dot_general(a, b, (((1,), (0,)), ((), ())), preferred_element_type=F32)


def dot_nt(a, b):
    return lax.dot_general(a, b, (((1,), (1,)), ((), ())), preferred_element_type=F32)


def place_kernel(peers, capacity, sub, owner_ref, coords_ref, elem_ref, upper_ref, send_ref, slot_ref, acc, carry):
    step = pl.program_id(0)

    @pl.when(step == 0)
    def _():
        acc[...] = jnp.zeros_like(acc)
        carry[...] = jnp.zeros_like(carry)

    block = owner_ref.shape[1]
    upper = upper_ref[...]
    peer_rows = lax.broadcasted_iota(jnp.int32, (peers, sub), 0)
    slots = []
    running = carry[:, 0:1]
    for part in range(block // sub):
        owner = owner_ref[:, part * sub : (part + 1) * sub]
        match = peer_rows == owner
        hot = match.astype(F32)
        earlier = dot(hot.astype(BF16), upper) + running
        slots.append(jnp.sum(jnp.where(match, earlier, 0.0), axis=0, keepdims=True))
        running = running + jnp.sum(hot, axis=1, keepdims=True)
    carry[...] = jnp.broadcast_to(running, carry.shape)
    slot = jnp.concatenate(slots, axis=1).astype(jnp.int32)
    slot_ref[...] = slot
    owner = jnp.broadcast_to(owner_ref[...], (8, block))
    hi, lo = split2(coords_ref[...])
    values = jnp.concatenate([hi, elem_ref[...].astype(F32), lo, jnp.zeros((1, block), F32)], axis=0)
    spread = jnp.concatenate([jnp.where(owner == p, values, 0.0) for p in range(peers)], axis=0).astype(BF16)
    for at in range(0, capacity, 256):
        width = min(256, capacity - at)
        rows = lax.broadcasted_iota(jnp.int32, (width, block), 0) + at
        hot = (rows == slot).astype(F32).astype(BF16)
        acc[:, at : at + width] += dot_nt(spread, hot)

    @pl.when(step == pl.num_programs(0) - 1)
    def _():
        for p in range(peers):
            both = acc[8 * p : 8 * p + 8]
            send_ref[p] = jnp.concatenate([both[0:3] + both[4:7], both[3:4]], axis=0)


def place(owner, coords, elem, peers, capacity):
    points = owner.shape[1]
    block, sub = math.gcd(points, 1024), math.gcd(points, 256)
    upper = np.triu(np.ones((sub, sub), np.float32), 1)
    return pl.pallas_call(
        functools.partial(place_kernel, peers, capacity, sub),
        grid=(points // block,),
        in_specs=[
            pl.BlockSpec((1, block), lambda i: (0, i)),
            pl.BlockSpec((3, block), lambda i: (0, i)),
            pl.BlockSpec((1, block), lambda i: (0, i)),
            pl.BlockSpec((sub, sub), lambda i: (0, 0)),
        ],
        out_specs=[
            pl.BlockSpec((peers, 4, capacity), lambda i: (0, 0, 0)),
            pl.BlockSpec((1, block), lambda i: (0, i)),
        ],
        out_shape=[
            jax.ShapeDtypeStruct((peers, 4, capacity), F32),
            jax.ShapeDtypeStruct((1, points), jnp.int32),
        ],
        scratch_shapes=[pltpu.VMEM((8 * peers, capacity), F32), pltpu.VMEM((peers, 128), F32)],
        compiler_params=pltpu.CompilerParams(dimension_semantics=("arbitrary",)),
        name="place",
    )(owner, coords, elem, jnp.asarray(upper, BF16))


def interp_chunks(elems, chunk, load, store, slots, stacked, const_ref):
    for at in range(0, slots, chunk):
        x = load(slice(at, at + chunk))
        weights = []
        for d in range(3):
            coord = jnp.broadcast_to(x[d : d + 1], (8, chunk))
            w = const_ref[:, 0:1] * (coord - const_ref[:, 1:2])
            for r in range(2, 8):
                w = w * (coord - const_ref[:, r : r + 1])
            weights.append(w)
        elem = jnp.broadcast_to(x[3:4], (8, chunk))
        hi, lo = split2(weights[2])
        picks = [elem == float(e) for e in range(elems)]
        a_hi = jnp.concatenate([jnp.where(pick, hi, 0.0) for pick in picks], axis=0).astype(BF16)
        a_lo = jnp.concatenate([jnp.where(pick, lo, 0.0) for pick in picks], axis=0).astype(BF16)
        summed = dot(stacked[...], jnp.concatenate([a_hi, a_lo, a_hi], axis=0))
        results = []
        for c in range(3):
            total = None
            for i in range(8):
                term = summed[64 * c + 8 * i : 64 * c + 8 * i + 8] * weights[0][i : i + 1]
                total = term if total is None else total + term
            results.append(jnp.sum(total * weights[1], axis=0, keepdims=True))
        store(slice(at, at + chunk), jnp.concatenate(results, axis=0))


def exchange_kernel(
    outer, inner, elems, chunk, send_ref, table_ref, const_ref, out_ref,
    stacked, arrived, replies, landed, go_out, go_in, back_out, back_in,
):
    peers = outer * inner
    slots = send_ref.shape[2]
    my_x, my_y = lax.axis_index("gx"), lax.axis_index("gy")
    me = my_x * inner + my_y

    def after(s):
        x, y = lax.rem(my_x + lax.rem(s, outer), outer), lax.rem(my_y + s // outer, inner)
        return x, y, x * inner + y

    def before(s):
        x = lax.rem(my_x + outer - lax.rem(s, outer), outer)
        y = lax.rem(my_y + inner - s // outer, inner)
        return x, y, x * inner + y

    barrier = pltpu.get_barrier_semaphore()

    @pl.loop(1, peers)
    def _(s):
        x, y, _ = after(s)
        pl.semaphore_signal(barrier, inc=1, device_id=(x, y), device_id_type=MESH)

    hi, lo = split2(table_ref[...])
    stacked[...] = jnp.concatenate([hi, hi, lo], axis=1).astype(BF16)
    pl.semaphore_wait(barrier, peers - 1)

    def outgoing(s):
        x, y, target = after(s)
        return pltpu.make_async_remote_copy(
            src_ref=send_ref.at[target], dst_ref=arrived.at[me],
            send_sem=go_out.at[target], recv_sem=go_in.at[me],
            device_id=(x, y), device_id_type=MESH,
        )

    def incoming(s):
        x, y, source = before(s)
        return pltpu.make_async_remote_copy(
            src_ref=send_ref.at[source], dst_ref=arrived.at[source],
            send_sem=go_out.at[source], recv_sem=go_in.at[source],
            device_id=(x, y), device_id_type=MESH,
        )

    def reply(s):
        x, y, source = before(s)
        return pltpu.make_async_remote_copy(
            src_ref=replies.at[source], dst_ref=landed.at[me],
            send_sem=back_out.at[source], recv_sem=back_in.at[me],
            device_id=(x, y), device_id_type=MESH,
        )

    def answer(s):
        x, y, target = after(s)
        return pltpu.make_async_remote_copy(
            src_ref=replies.at[target], dst_ref=landed.at[target],
            send_sem=back_out.at[target], recv_sem=back_in.at[target],
            device_id=(x, y), device_id_type=MESH,
        )

    @pl.loop(1, peers)
    def _(s):
        outgoing(s).start()

    def own_store(where, value):
        out_ref[me, :, where] = value

    interp_chunks(elems, chunk, lambda where: send_ref[me, :, where], own_store, slots, stacked, const_ref)

    @pl.loop(1, peers)
    def _(s):
        _, _, source = before(s)
        incoming(s).wait_recv()

        def store(where, value):
            replies[source, :, where] = value

        interp_chunks(elems, chunk, lambda where: arrived[source, :, where], store, slots, stacked, const_ref)

        @pl.when(s > 1)
        def _():
            reply(s - 1).start()

    @pl.loop(1, peers)
    def _(s):
        outgoing(s).wait_send()

    reply(peers - 1).start()

    @pl.loop(1, peers)
    def _(s):
        _, _, target = after(s)
        answer(s).wait_recv()
        out_ref[target] = landed[target]

    @pl.loop(1, peers)
    def _(s):
        reply(s).wait_send()


def exchange(send, table, outer, inner):
    peers, _, slots = send.shape
    elems = table.shape[1] // 8
    chunk = math.gcd(slots, 256)
    vmem = pl.BlockSpec(memory_space=pltpu.VMEM)
    return pl.pallas_call(
        functools.partial(exchange_kernel, outer, inner, elems, chunk),
        in_specs=[vmem] * 3,
        out_specs=vmem,
        out_shape=jax.ShapeDtypeStruct((peers, 3, slots), F32),
        scratch_shapes=[
            pltpu.VMEM((192, 3 * table.shape[1]), BF16),
            pltpu.VMEM((peers, 4, slots), F32),
            pltpu.VMEM((peers, 3, slots), F32),
            pltpu.VMEM((peers, 3, slots), F32),
        ] + [pltpu.SemaphoreType.DMA((peers,))] * 4,
        compiler_params=pltpu.CompilerParams(collective_id=0, has_side_effects=True),
        name="exchange",
    )(send, table, jnp.asarray(lagrange_constants()))


def finish_kernel(
    outer, inner, per_step, answers_ref, owner_ref, slot_ref, select_ref, index_ref, out_ref,
    halves, faces, below, above, send_sem, recv_sem,
):
    step = pl.program_id(0)
    peers = outer * inner
    capacity = answers_ref.shape[2]
    elems = out_ref.shape[1]
    me = lax.axis_index("gx") * inner + lax.axis_index("gy")
    up, down = lax.rem(me + 1, peers), lax.rem(me + peers - 1, peers)
    barrier = pltpu.get_barrier_semaphore()

    def place_of(device):
        return (device // inner, lax.rem(device, inner))

    @pl.when(step == 0)
    def _():
        for device in (up, down):
            pl.semaphore_signal(barrier, inc=1, device_id=place_of(device), device_id_type=MESH)
        gap = jnp.zeros((1, capacity), F32)
        for p in range(0, peers, 2):
            rows = []
            for q in (p, p + 1):
                hi, lo = split2(answers_ref[q])
                rows += [hi, gap, lo, gap]
            halves[8 * p : 8 * p + 16] = jnp.concatenate(rows, axis=0).astype(BF16)

    for at in range(per_step):
        nodes = slice(512 * at, 512 * at + 512)
        slot = slot_ref[:, nodes]
        rows = lax.broadcasted_iota(jnp.int32, (capacity, 512), 0)
        hot = (rows == slot).astype(F32).astype(BF16)
        picked = dot(halves[...], hot)
        owner = jnp.broadcast_to(owner_ref[:, nodes], (8, 512))
        total = jnp.zeros((8, 512), F32)
        for p in range(peers):
            total = total + jnp.where(owner == p, picked[8 * p : 8 * p + 8], 0.0)
        for c in range(3):
            out_ref[c, pl.ds(step * per_step + at, 1), :] = total[c : c + 1] + total[c + 4 : c + 5]

    @pl.when(step == pl.num_programs(0) - 1)
    def _():
        sel = select_ref[...]
        for c in range(3):
            hi, lo = split2(out_ref[c])
            mid, low = split2(lo)
            faces[c] = dot(hi.astype(BF16), sel) + dot(mid.astype(BF16), sel) + dot(low.astype(BF16), sel)
        index = index_ref[...]
        columns = lax.broadcasted_iota(jnp.int32, (6 * elems, 3 * elems), 1)
        picker = (columns == index).astype(F32).astype(BF16)
        present = (index >= 0).astype(F32)
        pl.semaphore_wait(barrier, 2)
        copies = [
            pltpu.make_async_remote_copy(
                src_ref=faces, dst_ref=land, send_sem=send_sem.at[k], recv_sem=recv_sem.at[k],
                device_id=place_of(device), device_id_type=MESH,
            )
            for k, (device, land) in enumerate(((up, below), (down, above)))
        ]
        for copy in copies:
            copy.start()
        for copy in copies:
            copy.wait()
        for c in range(3):
            own = faces[c]
            extended = jnp.concatenate([below[c], own, above[c]], axis=0)
            hi, lo = split2(extended)
            across = dot(picker, hi.astype(BF16)) + dot(picker, lo.astype(BF16))
            changes = []
            for f in range(6):
                g = f ^ 1
                rows = slice(f * elems, (f + 1) * elems)
                other = across[rows, 64 * g : 64 * g + 64]
                changes.append(0.5 * (other - present[rows] * own[:, 64 * f : 64 * f + 64]))
            hi, lo = split2(jnp.concatenate(changes, axis=1))
            out_ref[c] += dot_nt(hi.astype(BF16), sel) + dot_nt(lo.astype(BF16), sel)


def finish(answers, owner, slot, index, elems, outer, inner):
    peers, _, capacity = answers.shape
    points = owner.shape[1]
    per_step = math.gcd(elems, 2)
    block = per_step * 512
    return pl.pallas_call(
        functools.partial(finish_kernel, outer, inner, per_step),
        grid=(points // block,),
        in_specs=[
            pl.BlockSpec(answers.shape, lambda i: (0, 0, 0)),
            pl.BlockSpec((1, block), lambda i: (0, i)),
            pl.BlockSpec((1, block), lambda i: (0, i)),
            pl.BlockSpec((512, 384), lambda i: (0, 0)),
            pl.BlockSpec(index.shape, lambda i: (0, 0)),
        ],
        out_specs=pl.BlockSpec((3, elems, 512), lambda i: (0, 0, 0)),
        out_shape=jax.ShapeDtypeStruct((3, elems, 512), F32),
        scratch_shapes=[pltpu.VMEM((8 * peers, capacity), BF16)]
        + [pltpu.VMEM((3, elems, 384), F32)] * 3
        + [pltpu.SemaphoreType.DMA((2,))] * 2,
        compiler_params=pltpu.CompilerParams(
            dimension_semantics=("arbitrary",), collective_id=1, has_side_effects=True
        ),
        name="finish",
    )(answers, owner, slot, jnp.asarray(face_selector(), BF16), index)


def local(velocity, depart, owner_rank, owner_element_index, neighbours):
    outer, inner = lax.axis_size("gx"), lax.axis_size("gy")
    peers = outer * inner
    elems = velocity.shape[1]
    points = depart.shape[1]
    capacity = 2 * points // peers
    owner = owner_rank.reshape(1, points)
    table = velocity.reshape(3, elems, 64, 8).transpose(0, 2, 1, 3).reshape(192, elems * 8)
    send, slot = place(owner, depart, owner_element_index.reshape(1, points), peers, capacity)
    answers = exchange(send, table, outer, inner)
    device_id = lax.axis_index("gx") * inner + lax.axis_index("gy")
    index = jnp.where(neighbours >= 0, neighbours - (device_id - 1) * elems, -1)
    return finish(answers, owner, slot, index.reshape(6 * elems, 1), elems, outer, inner)


def solution(mesh):
    placed = (
        P(None, ("gx", "gy"), None),
        P(None, ("gx", "gy")),
        P(("gx", "gy"), None),
        P(("gx", "gy")),
        P(None, ("gx", "gy")),
    )
    return jax.shard_map(
        local, mesh=mesh, in_specs=placed, out_specs=P(None, ("gx", "gy"), None), check_vma=False
    )
```

```python
import functools
import math

import jax
import jax.numpy as jnp
import numpy as np
from jax import lax
from jax.experimental import pallas as pl
from jax.experimental.pallas import tpu as pltpu
from jax.sharding import PartitionSpec as P

GLL_POINTS = np.array(
    [
        -1.0,
        -0.8717401485096066,
        -0.5917001814331423,
        -0.2092992179024789,
        0.2092992179024789,
        0.5917001814331423,
        0.8717401485096066,
        1.0,
    ]
)
F32, BF16 = jnp.float32, jnp.bfloat16
MESH = pl.DeviceIdType.MESH


def lagrange_constants():
    table = np.zeros((8, 128))
    for i in range(8):
        table[i, 0] = 1.0 / np.prod([GLL_POINTS[i] - GLL_POINTS[m] for m in range(8) if m != i])
        for r in range(1, 8):
            table[i, r] = GLL_POINTS[(i + r) % 8]
    return table.astype(np.float32)


def face_selector():
    cube = np.arange(512).reshape(8, 8, 8)
    faces = [cube[0], cube[7], cube[:, 0], cube[:, 7], cube[:, :, 0], cube[:, :, 7]]
    nodes = np.concatenate([face.reshape(-1) for face in faces])
    return (np.arange(512)[:, None] == nodes[None, :]).astype(np.float32)


def split2(x):
    hi = x.astype(BF16).astype(F32)
    return hi, x - hi


def dot(a, b):
    return lax.dot_general(a, b, (((1,), (0,)), ((), ())), preferred_element_type=F32)


def dot_nt(a, b):
    return lax.dot_general(a, b, (((1,), (1,)), ((), ())), preferred_element_type=F32)


def one_hot_rows(slot, capacity):
    width = slot.shape[1]
    rows = lax.broadcasted_iota(jnp.int32, (capacity, 128), 0).astype(jnp.int16)
    rows = jnp.concatenate([rows] * (width // 128), axis=1)
    slots = jnp.broadcast_to(slot, (16, width)).astype(jnp.int16)
    slots = jnp.concatenate([slots] * (capacity // 16), axis=0)
    return jnp.where(rows == slots, jnp.array(1, BF16), jnp.array(0, BF16))


def place_step(peers, capacity, sub, owner_ref, coords_ref, elem_ref, upper_ref, slot_ref, acc, carry):
    @pl.when(pl.program_id(0) == 0)
    def _():
        acc[...] = jnp.zeros_like(acc)
        carry[...] = jnp.zeros_like(carry)

    block = owner_ref.shape[1]
    upper = upper_ref[...]
    peer_rows = lax.broadcasted_iota(jnp.int32, (peers, sub), 0)
    slots = []
    running = carry[:, 0:1]
    for part in range(block // sub):
        owner = owner_ref[:, part * sub : (part + 1) * sub]
        match = peer_rows == owner
        hot = match.astype(F32)
        earlier = dot(hot.astype(BF16), upper) + running
        slots.append(jnp.sum(jnp.where(match, earlier, 0.0), axis=0, keepdims=True))
        running = running + jnp.sum(hot, axis=1, keepdims=True)
    carry[...] = jnp.broadcast_to(running, carry.shape)
    slot = jnp.concatenate(slots, axis=1).astype(jnp.int32)
    slot_ref[...] = slot
    owner = jnp.broadcast_to(owner_ref[...], (8, block))
    hi, lo = split2(coords_ref[...])
    values = jnp.concatenate([hi, elem_ref[...].astype(F32), lo, jnp.zeros((1, block), F32)], axis=0)
    spread = jnp.concatenate([jnp.where(owner == p, values, 0.0) for p in range(peers)], axis=0).astype(BF16)
    rows = lax.broadcasted_iota(jnp.int32, (capacity, block), 0)
    acc[...] += dot_nt((rows == slot).astype(F32).astype(BF16), spread)


def interp_chunks(elems, chunk, load, store, slots, stacked, const_ref):
    for at in range(0, slots, chunk):
        x = load(slice(at, at + chunk))
        weights = []
        for d in range(3):
            coord = jnp.broadcast_to(x[d : d + 1], (8, chunk))
            w = const_ref[:, 0:1] * (coord - const_ref[:, 1:2])
            for r in range(2, 8):
                w = w * (coord - const_ref[:, r : r + 1])
            weights.append(w)
        elem = jnp.broadcast_to(x[3:4], (8, chunk))
        hi, lo = split2(weights[2])
        picks = [elem == float(e) for e in range(elems)]
        a_hi = jnp.concatenate([jnp.where(pick, hi, 0.0) for pick in picks], axis=0).astype(BF16)
        a_lo = jnp.concatenate([jnp.where(pick, lo, 0.0) for pick in picks], axis=0).astype(BF16)
        summed = dot(stacked[...], jnp.concatenate([a_hi, a_lo, a_hi], axis=0))
        results = []
        for c in range(3):
            total = None
            for i in range(8):
                term = summed[64 * c + 8 * i : 64 * c + 8 * i + 8] * weights[0][i : i + 1]
                total = term if total is None else total + term
            results.append(jnp.sum(total * weights[1], axis=0, keepdims=True))
        store(slice(at, at + chunk), jnp.concatenate(results, axis=0))


def exchange_kernel(
    outer, inner, elems, chunk, sub, owner_ref, coords_ref, elem_ref, upper_ref, table_ref, const_ref,
    out_ref, slot_ref, acc, carry, send_ref, stacked, arrived, replies, landed, go_out, go_in, back_out, back_in,
):
    peers = outer * inner
    slots = out_ref.shape[2]
    my_x, my_y = lax.axis_index("gx"), lax.axis_index("gy")
    me = my_x * inner + my_y

    def after(s):
        x, y = lax.rem(my_x + lax.rem(s, outer), outer), lax.rem(my_y + s // outer, inner)
        return x, y, x * inner + y

    def before(s):
        x = lax.rem(my_x + outer - lax.rem(s, outer), outer)
        y = lax.rem(my_y + inner - s // outer, inner)
        return x, y, x * inner + y

    barrier = pltpu.get_barrier_semaphore()

    @pl.when(pl.program_id(0) == 0)
    def _():
        @pl.loop(1, peers)
        def _(s):
            x, y, _ = after(s)
            pl.semaphore_signal(barrier, inc=1, device_id=(x, y), device_id_type=MESH)

        hi, lo = split2(table_ref[...])
        stacked[...] = jnp.concatenate([hi, hi, lo], axis=1).astype(BF16)

    place_step(peers, slots, sub, owner_ref, coords_ref, elem_ref, upper_ref, slot_ref, acc, carry)

    def outgoing(s):
        x, y, target = after(s)
        return pltpu.make_async_remote_copy(
            src_ref=send_ref.at[target], dst_ref=arrived.at[me],
            send_sem=go_out.at[target], recv_sem=go_in.at[me],
            device_id=(x, y), device_id_type=MESH,
        )

    def incoming(s):
        x, y, source = before(s)
        return pltpu.make_async_remote_copy(
            src_ref=send_ref.at[source], dst_ref=arrived.at[source],
            send_sem=go_out.at[source], recv_sem=go_in.at[source],
            device_id=(x, y), device_id_type=MESH,
        )

    def reply(s):
        x, y, source = before(s)
        return pltpu.make_async_remote_copy(
            src_ref=replies.at[source], dst_ref=landed.at[me],
            send_sem=back_out.at[source], recv_sem=back_in.at[me],
            device_id=(x, y), device_id_type=MESH,
        )

    def answer(s):
        x, y, target = after(s)
        return pltpu.make_async_remote_copy(
            src_ref=replies.at[target], dst_ref=landed.at[target],
            send_sem=back_out.at[target], recv_sem=back_in.at[target],
            device_id=(x, y), device_id_type=MESH,
        )

    @pl.when(pl.program_id(0) == pl.num_programs(0) - 1)
    def _():
        turned = acc[...].T
        for p in range(peers):
            both = turned[8 * p : 8 * p + 8]
            send_ref[p] = jnp.concatenate([both[0:3] + both[4:7], both[3:4]], axis=0)
        pl.semaphore_wait(barrier, peers - 1)

        @pl.loop(1, peers)
        def _(s):
            outgoing(s).start()

        def own_store(where, value):
            out_ref[me, :, where] = value

        interp_chunks(elems, chunk, lambda where: send_ref[me, :, where], own_store, slots, stacked, const_ref)

        @pl.loop(1, peers)
        def _(s):
            _, _, source = before(s)
            incoming(s).wait_recv()

            def store(where, value):
                replies[source, :, where] = value

            interp_chunks(elems, chunk, lambda where: arrived[source, :, where], store, slots, stacked, const_ref)

            @pl.when(s > 1)
            def _():
                reply(s - 1).start()

        @pl.loop(1, peers)
        def _(s):
            outgoing(s).wait_send()

        reply(peers - 1).start()

        @pl.loop(1, peers)
        def _(s):
            _, _, target = after(s)
            answer(s).wait_recv()
            out_ref[target] = landed[target]

        @pl.loop(1, peers)
        def _(s):
            reply(s).wait_send()


def exchange(owner, coords, elem, table, outer, inner, capacity):
    peers = outer * inner
    points = owner.shape[1]
    elems = table.shape[1] // 8
    chunk = math.gcd(capacity, 256)
    block, sub = math.gcd(points, 4096), math.gcd(points, 256)
    upper = np.triu(np.ones((sub, sub), np.float32), 1)
    whole = lambda i: (0, 0)
    return pl.pallas_call(
        functools.partial(exchange_kernel, outer, inner, elems, chunk, sub),
        grid=(points // block,),
        in_specs=[
            pl.BlockSpec((1, block), lambda i: (0, i)),
            pl.BlockSpec((3, block), lambda i: (0, i)),
            pl.BlockSpec((1, block), lambda i: (0, i)),
            pl.BlockSpec((sub, sub), whole),
            pl.BlockSpec(table.shape, whole),
            pl.BlockSpec((8, 128), whole),
        ],
        out_specs=[
            pl.BlockSpec((peers, 3, capacity), lambda i: (0, 0, 0)),
            pl.BlockSpec((1, block), lambda i: (0, i)),
        ],
        out_shape=[
            jax.ShapeDtypeStruct((peers, 3, capacity), F32),
            jax.ShapeDtypeStruct((1, points), jnp.int32),
        ],
        scratch_shapes=[
            pltpu.VMEM((capacity, 8 * peers), F32),
            pltpu.VMEM((peers, 128), F32),
            pltpu.VMEM((peers, 4, capacity), F32),
            pltpu.VMEM((192, 3 * table.shape[1]), BF16),
            pltpu.VMEM((peers, 4, capacity), F32),
            pltpu.VMEM((peers, 3, capacity), F32),
            pltpu.VMEM((peers, 3, capacity), F32),
        ] + [pltpu.SemaphoreType.DMA((peers,))] * 4,
        compiler_params=pltpu.CompilerParams(
            dimension_semantics=("arbitrary",), collective_id=0, has_side_effects=True
        ),
        name="exchange",
    )(owner, coords, elem, jnp.asarray(upper, BF16), table, jnp.asarray(lagrange_constants()))


def finish_kernel(
    outer, inner, per_step, answers_ref, owner_ref, slot_ref, select_ref, index_ref, out_ref,
    halves, faces, below, above, send_sem, recv_sem,
):
    step = pl.program_id(0)
    peers = outer * inner
    capacity = answers_ref.shape[2]
    elems = out_ref.shape[1]
    me = lax.axis_index("gx") * inner + lax.axis_index("gy")
    up, down = lax.rem(me + 1, peers), lax.rem(me + peers - 1, peers)
    barrier = pltpu.get_barrier_semaphore()

    def place_of(device):
        return (device // inner, lax.rem(device, inner))

    @pl.when(step == 0)
    def _():
        for device in (up, down):
            pl.semaphore_signal(barrier, inc=1, device_id=place_of(device), device_id_type=MESH)
        for c in range(3):
            hi, lo = split2(answers_ref[:, c, :])
            halves[peers * c : peers * (c + 1)] = hi.astype(BF16)
            halves[peers * (c + 3) : peers * (c + 4)] = lo.astype(BF16)

    for at in range(per_step):
        nodes = slice(512 * at, 512 * at + 512)
        picked = dot(halves[...], one_hot_rows(slot_ref[:, nodes], capacity))
        match = lax.broadcasted_iota(jnp.int32, (peers, 512), 0) == owner_ref[:, nodes]
        for c in range(3):
            both = picked[peers * c : peers * (c + 1)] + picked[peers * (c + 3) : peers * (c + 4)]
            value = jnp.sum(jnp.where(match, both, 0.0), axis=0, keepdims=True)
            out_ref[c, pl.ds(step * per_step + at, 1), :] = value

    @pl.when(step == pl.num_programs(0) - 1)
    def _():
        sel = select_ref[...]
        for c in range(3):
            hi, lo = split2(out_ref[c])
            mid, low = split2(lo)
            faces[c] = dot(hi.astype(BF16), sel) + dot(mid.astype(BF16), sel) + dot(low.astype(BF16), sel)
        index = index_ref[...]
        columns = lax.broadcasted_iota(jnp.int32, (6 * elems, 3 * elems), 1)
        picker = (columns == index).astype(F32).astype(BF16)
        present = (index >= 0).astype(F32)
        pl.semaphore_wait(barrier, 2)
        copies = [
            pltpu.make_async_remote_copy(
                src_ref=faces, dst_ref=land, send_sem=send_sem.at[k], recv_sem=recv_sem.at[k],
                device_id=place_of(device), device_id_type=MESH,
            )
            for k, (device, land) in enumerate(((up, below), (down, above)))
        ]
        for copy in copies:
            copy.start()
        for copy in copies:
            copy.wait()
        for c in range(3):
            own = faces[c]
            extended = jnp.concatenate([below[c], own, above[c]], axis=0)
            hi, lo = split2(extended)
            across = dot(picker, hi.astype(BF16)) + dot(picker, lo.astype(BF16))
            changes = []
            for f in range(6):
                g = f ^ 1
                rows = slice(f * elems, (f + 1) * elems)
                other = across[rows, 64 * g : 64 * g + 64]
                changes.append(0.5 * (other - present[rows] * own[:, 64 * f : 64 * f + 64]))
            hi, lo = split2(jnp.concatenate(changes, axis=1))
            out_ref[c] += dot_nt(hi.astype(BF16), sel) + dot_nt(lo.astype(BF16), sel)


def finish(answers, owner, slot, index, elems, outer, inner):
    peers, _, capacity = answers.shape
    points = owner.shape[1]
    per_step = math.gcd(elems, 8)
    block = per_step * 512
    return pl.pallas_call(
        functools.partial(finish_kernel, outer, inner, per_step),
        grid=(points // block,),
        in_specs=[
            pl.BlockSpec(answers.shape, lambda i: (0, 0, 0)),
            pl.BlockSpec((1, block), lambda i: (0, i)),
            pl.BlockSpec((1, block), lambda i: (0, i)),
            pl.BlockSpec((512, 384), lambda i: (0, 0)),
            pl.BlockSpec(index.shape, lambda i: (0, 0)),
        ],
        out_specs=pl.BlockSpec((3, elems, 512), lambda i: (0, 0, 0)),
        out_shape=jax.ShapeDtypeStruct((3, elems, 512), F32),
        scratch_shapes=[pltpu.VMEM((6 * peers, capacity), BF16)]
        + [pltpu.VMEM((3, elems, 384), F32)] * 3
        + [pltpu.SemaphoreType.DMA((2,))] * 2,
        compiler_params=pltpu.CompilerParams(
            dimension_semantics=("arbitrary",), collective_id=1, has_side_effects=True
        ),
        name="finish",
    )(answers, owner, slot, jnp.asarray(face_selector(), BF16), index)


def local(velocity, depart, owner_rank, owner_element_index, neighbours):
    outer, inner = lax.axis_size("gx"), lax.axis_size("gy")
    peers = outer * inner
    elems = velocity.shape[1]
    points = depart.shape[1]
    capacity = 2 * points // peers
    owner = owner_rank.reshape(1, points)
    table = velocity.reshape(3, elems, 64, 8).transpose(0, 2, 1, 3).reshape(192, elems * 8)
    elem = owner_element_index.reshape(1, points)
    answers, slot = exchange(owner, depart, elem, table, outer, inner, capacity)
    device_id = lax.axis_index("gx") * inner + lax.axis_index("gy")
    index = jnp.where(neighbours >= 0, neighbours - (device_id - 1) * elems, -1)
    return finish(answers, owner, slot, index.reshape(6 * elems, 1), elems, outer, inner)


def solution(mesh):
    placed = (
        P(None, ("gx", "gy"), None),
        P(None, ("gx", "gy")),
        P(("gx", "gy"), None),
        P(("gx", "gy")),
        P(None, ("gx", "gy")),
    )
    return jax.shard_map(
        local, mesh=mesh, in_specs=placed, out_specs=P(None, ("gx", "gy"), None), check_vma=False
    )
```

```python
import functools
import math

import jax
import jax.numpy as jnp
import numpy as np
from jax import lax
from jax.experimental import pallas as pl
from jax.experimental.pallas import tpu as pltpu
from jax.sharding import PartitionSpec as P

GLL_POINTS = np.array(
    [
        -1.0,
        -0.8717401485096066,
        -0.5917001814331423,
        -0.2092992179024789,
        0.2092992179024789,
        0.5917001814331423,
        0.8717401485096066,
        1.0,
    ]
)
F32, BF16 = jnp.float32, jnp.bfloat16
MESH = pl.DeviceIdType.MESH


def lagrange_constants():
    table = np.zeros((8, 128))
    for i in range(8):
        table[i, 0] = 1.0 / np.prod([GLL_POINTS[i] - GLL_POINTS[m] for m in range(8) if m != i])
        for r in range(1, 8):
            table[i, r] = GLL_POINTS[(i + r) % 8]
    return table.astype(np.float32)


def face_selector():
    cube = np.arange(512).reshape(8, 8, 8)
    faces = [cube[0], cube[7], cube[:, 0], cube[:, 7], cube[:, :, 0], cube[:, :, 7]]
    nodes = np.concatenate([face.reshape(-1) for face in faces])
    return (np.arange(512)[:, None] == nodes[None, :]).astype(np.float32)


def split2(x):
    hi = x.astype(BF16).astype(F32)
    return hi, x - hi


def dot(a, b):
    return lax.dot_general(a, b, (((1,), (0,)), ((), ())), preferred_element_type=F32)


def dot_nt(a, b):
    return lax.dot_general(a, b, (((1,), (1,)), ((), ())), preferred_element_type=F32)


def one_hot_rows(slot, capacity):
    width = slot.shape[1]
    rows = lax.broadcasted_iota(jnp.int32, (capacity, 128), 0).astype(jnp.int16)
    rows = jnp.concatenate([rows] * (width // 128), axis=1)
    slots = jnp.broadcast_to(slot, (16, width)).astype(jnp.int16)
    slots = jnp.concatenate([slots] * (capacity // 16), axis=0)
    return jnp.where(rows == slots, jnp.array(1, BF16), jnp.array(0, BF16))


def place_step(peers, capacity, sub, owner_ref, coords_ref, elem_ref, upper_ref, slot_ref, acc, carry):
    @pl.when(pl.program_id(0) == 0)
    def _():
        acc[...] = jnp.zeros_like(acc)
        carry[...] = jnp.zeros_like(carry)

    block = owner_ref.shape[1]
    upper = upper_ref[...]
    peer_rows = lax.broadcasted_iota(jnp.int32, (peers, sub), 0)
    slots = []
    running = carry[:, 0:1]
    for part in range(block // sub):
        owner = owner_ref[:, part * sub : (part + 1) * sub]
        match = peer_rows == owner
        hot = match.astype(F32)
        earlier = dot(hot.astype(BF16), upper) + running
        slots.append(jnp.sum(jnp.where(match, earlier, 0.0), axis=0, keepdims=True))
        running = running + jnp.sum(hot, axis=1, keepdims=True)
    carry[...] = jnp.broadcast_to(running, carry.shape)
    slot = jnp.concatenate(slots, axis=1).astype(jnp.int32)
    slot_ref[...] = slot
    owner = jnp.broadcast_to(owner_ref[...], (8, block))
    hi, lo = split2(coords_ref[...])
    values = jnp.concatenate([hi, elem_ref[...].astype(F32), lo, jnp.zeros((1, block), F32)], axis=0)
    spread = jnp.concatenate([jnp.where(owner == p, values, 0.0) for p in range(peers)], axis=0).astype(BF16)
    rows = lax.broadcasted_iota(jnp.int32, (capacity, block), 0)
    acc[...] += dot_nt((rows == slot).astype(F32).astype(BF16), spread)


def interp_chunks(elems, chunk, load, store, slots, stacked, const_ref):
    for at in range(0, slots, chunk):
        x = load(slice(at, at + chunk))
        weights = []
        for d in range(3):
            coord = jnp.broadcast_to(x[d : d + 1], (8, chunk))
            w = const_ref[:, 0:1] * (coord - const_ref[:, 1:2])
            for r in range(2, 8):
                w = w * (coord - const_ref[:, r : r + 1])
            weights.append(w)
        elem = jnp.broadcast_to(x[3:4], (8, chunk))
        hi, lo = split2(weights[2])
        picks = [elem == float(e) for e in range(elems)]
        a_hi = jnp.concatenate([jnp.where(pick, hi, 0.0) for pick in picks], axis=0).astype(BF16)
        a_lo = jnp.concatenate([jnp.where(pick, lo, 0.0) for pick in picks], axis=0).astype(BF16)
        summed = dot(stacked[...], jnp.concatenate([a_hi, a_lo, a_hi], axis=0))
        results = []
        for c in range(3):
            total = None
            for i in range(8):
                term = summed[64 * c + 8 * i : 64 * c + 8 * i + 8] * weights[0][i : i + 1]
                total = term if total is None else total + term
            results.append(jnp.sum(total * weights[1], axis=0, keepdims=True))
        store(slice(at, at + chunk), jnp.concatenate(results, axis=0))


def exchange_kernel(
    outer, inner, elems, chunk, sub, owner_ref, coords_ref, elem_ref, upper_ref, table_ref, const_ref,
    out_ref, slot_ref, acc, carry, send_ref, stacked, arrived, replies, landed, go_out, go_in, back_out, back_in,
):
    peers = outer * inner
    slots = out_ref.shape[2]
    my_x, my_y = lax.axis_index("gx"), lax.axis_index("gy")
    me = my_x * inner + my_y

    def after(s):
        x, y = lax.rem(my_x + lax.rem(s, outer), outer), lax.rem(my_y + s // outer, inner)
        return x, y, x * inner + y

    def before(s):
        x = lax.rem(my_x + outer - lax.rem(s, outer), outer)
        y = lax.rem(my_y + inner - s // outer, inner)
        return x, y, x * inner + y

    barrier = pltpu.get_barrier_semaphore()

    @pl.when(pl.program_id(0) == 0)
    def _():
        @pl.loop(1, peers)
        def _(s):
            x, y, _ = after(s)
            pl.semaphore_signal(barrier, inc=1, device_id=(x, y), device_id_type=MESH)

        hi, lo = split2(table_ref[...])
        stacked[...] = jnp.concatenate([hi, hi, lo], axis=1).astype(BF16)

    place_step(peers, slots, sub, owner_ref, coords_ref, elem_ref, upper_ref, slot_ref, acc, carry)

    def outgoing(s):
        x, y, target = after(s)
        return pltpu.make_async_remote_copy(
            src_ref=send_ref.at[target], dst_ref=arrived.at[me],
            send_sem=go_out.at[target], recv_sem=go_in.at[me],
            device_id=(x, y), device_id_type=MESH,
        )

    def incoming(s):
        x, y, source = before(s)
        return pltpu.make_async_remote_copy(
            src_ref=send_ref.at[source], dst_ref=arrived.at[source],
            send_sem=go_out.at[source], recv_sem=go_in.at[source],
            device_id=(x, y), device_id_type=MESH,
        )

    def reply(s):
        x, y, source = before(s)
        return pltpu.make_async_remote_copy(
            src_ref=replies.at[source], dst_ref=landed.at[me],
            send_sem=back_out.at[source], recv_sem=back_in.at[me],
            device_id=(x, y), device_id_type=MESH,
        )

    def answer(s):
        x, y, target = after(s)
        return pltpu.make_async_remote_copy(
            src_ref=replies.at[target], dst_ref=landed.at[target],
            send_sem=back_out.at[target], recv_sem=back_in.at[target],
            device_id=(x, y), device_id_type=MESH,
        )

    @pl.when(pl.program_id(0) == pl.num_programs(0) - 1)
    def _():
        turned = acc[...].T
        for p in range(peers):
            both = turned[8 * p : 8 * p + 8]
            send_ref[p] = jnp.concatenate([both[0:3] + both[4:7], both[3:4]], axis=0)
        pl.semaphore_wait(barrier, peers - 1)

        @pl.loop(1, peers)
        def _(s):
            outgoing(s).start()

        def own_store(where, value):
            out_ref[me, :, where] = value

        interp_chunks(elems, chunk, lambda where: send_ref[me, :, where], own_store, slots, stacked, const_ref)

        @pl.loop(1, peers)
        def _(s):
            _, _, source = before(s)
            incoming(s).wait_recv()

            def store(where, value):
                replies[source, :, where] = value

            interp_chunks(elems, chunk, lambda where: arrived[source, :, where], store, slots, stacked, const_ref)

            @pl.when(s > 1)
            def _():
                reply(s - 1).start()

        @pl.loop(1, peers)
        def _(s):
            outgoing(s).wait_send()

        reply(peers - 1).start()

        @pl.loop(1, peers)
        def _(s):
            _, _, target = after(s)
            answer(s).wait_recv()
            out_ref[target] = landed[target]

        @pl.loop(1, peers)
        def _(s):
            reply(s).wait_send()


def exchange(owner, coords, elem, table, outer, inner, capacity):
    peers = outer * inner
    points = owner.shape[1]
    elems = table.shape[1] // 8
    chunk = math.gcd(capacity, 256)
    block, sub = math.gcd(points, 4096), math.gcd(points, 256)
    upper = np.triu(np.ones((sub, sub), np.float32), 1)
    whole = lambda i: (0, 0)
    return pl.pallas_call(
        functools.partial(exchange_kernel, outer, inner, elems, chunk, sub),
        grid=(points // block,),
        in_specs=[
            pl.BlockSpec((1, block), lambda i: (0, i)),
            pl.BlockSpec((3, block), lambda i: (0, i)),
            pl.BlockSpec((1, block), lambda i: (0, i)),
            pl.BlockSpec((sub, sub), whole),
            pl.BlockSpec(table.shape, whole),
            pl.BlockSpec((8, 128), whole),
        ],
        out_specs=[
            pl.BlockSpec((peers, 3, capacity), lambda i: (0, 0, 0)),
            pl.BlockSpec((1, block), lambda i: (0, i)),
        ],
        out_shape=[
            jax.ShapeDtypeStruct((peers, 3, capacity), F32),
            jax.ShapeDtypeStruct((1, points), jnp.int32),
        ],
        scratch_shapes=[
            pltpu.VMEM((capacity, 8 * peers), F32),
            pltpu.VMEM((peers, 128), F32),
            pltpu.VMEM((peers, 4, capacity), F32),
            pltpu.VMEM((192, 3 * table.shape[1]), BF16),
            pltpu.VMEM((peers, 4, capacity), F32),
            pltpu.VMEM((peers, 3, capacity), F32),
            pltpu.VMEM((peers, 3, capacity), F32),
        ] + [pltpu.SemaphoreType.DMA((peers,))] * 4,
        compiler_params=pltpu.CompilerParams(
            dimension_semantics=("arbitrary",), collective_id=0, has_side_effects=True
        ),
        name="exchange",
    )(owner, coords, elem, jnp.asarray(upper, BF16), table, jnp.asarray(lagrange_constants()))


def finish_kernel(
    outer, inner, per_step, answers_ref, owner_ref, slot_ref, select_ref, index_ref, out_ref,
    halves, faces, below, above, send_sem, recv_sem,
):
    step = pl.program_id(0)
    peers = outer * inner
    capacity = answers_ref.shape[2]
    elems = out_ref.shape[1]
    me = lax.axis_index("gx") * inner + lax.axis_index("gy")
    up, down = lax.rem(me + 1, peers), lax.rem(me + peers - 1, peers)
    barrier = pltpu.get_barrier_semaphore()

    def place_of(device):
        return (device // inner, lax.rem(device, inner))

    @pl.when(step == 0)
    def _():
        for device in (up, down):
            pl.semaphore_signal(barrier, inc=1, device_id=place_of(device), device_id_type=MESH)
        for c in range(3):
            hi, lo = split2(answers_ref[:, c, :])
            halves[peers * c : peers * (c + 1)] = hi.astype(BF16)
            halves[peers * (c + 3) : peers * (c + 4)] = lo.astype(BF16)

    for at in range(per_step):
        nodes = slice(512 * at, 512 * at + 512)
        picked = dot(halves[...], one_hot_rows(slot_ref[:, nodes], capacity))
        match = lax.broadcasted_iota(jnp.int32, (peers, 512), 0) == owner_ref[:, nodes]
        for c in range(3):
            both = picked[peers * c : peers * (c + 1)] + picked[peers * (c + 3) : peers * (c + 4)]
            value = jnp.sum(jnp.where(match, both, 0.0), axis=0, keepdims=True)
            out_ref[c, pl.ds(step * per_step + at, 1), :] = value

    @pl.when(step == pl.num_programs(0) - 1)
    def _():
        sel = select_ref[...]
        copies = [
            [
                pltpu.make_async_remote_copy(
                    src_ref=faces.at[c], dst_ref=land.at[c],
                    send_sem=send_sem.at[2 * c + k], recv_sem=recv_sem.at[2 * c + k],
                    device_id=place_of(device), device_id_type=MESH,
                )
                for k, (device, land) in enumerate(((up, below), (down, above)))
            ]
            for c in range(3)
        ]
        pl.semaphore_wait(barrier, 2)
        for c in range(3):
            hi, lo = split2(out_ref[c])
            mid, low = split2(lo)
            faces[c] = dot(hi.astype(BF16), sel) + dot(mid.astype(BF16), sel) + dot(low.astype(BF16), sel)
            if c > 0:
                for copy in copies[c - 1]:
                    copy.start()
        index = index_ref[...]
        columns = lax.broadcasted_iota(jnp.int32, (6 * elems, 3 * elems), 1)
        picker = (columns == index).astype(F32).astype(BF16)
        present = (index >= 0).astype(F32)
        for copy in copies[2]:
            copy.start()
        for c in range(3):
            for copy in copies[c]:
                copy.wait()
            own = faces[c]
            extended = jnp.concatenate([below[c], own, above[c]], axis=0)
            hi, lo = split2(extended)
            across = dot(picker, hi.astype(BF16)) + dot(picker, lo.astype(BF16))
            changes = []
            for f in range(6):
                g = f ^ 1
                rows = slice(f * elems, (f + 1) * elems)
                other = across[rows, 64 * g : 64 * g + 64]
                changes.append(0.5 * (other - present[rows] * own[:, 64 * f : 64 * f + 64]))
            hi, lo = split2(jnp.concatenate(changes, axis=1))
            out_ref[c] += dot_nt(hi.astype(BF16), sel) + dot_nt(lo.astype(BF16), sel)


def finish(answers, owner, slot, index, elems, outer, inner):
    peers, _, capacity = answers.shape
    points = owner.shape[1]
    per_step = math.gcd(elems, 8)
    block = per_step * 512
    return pl.pallas_call(
        functools.partial(finish_kernel, outer, inner, per_step),
        grid=(points // block,),
        in_specs=[
            pl.BlockSpec(answers.shape, lambda i: (0, 0, 0)),
            pl.BlockSpec((1, block), lambda i: (0, i)),
            pl.BlockSpec((1, block), lambda i: (0, i)),
            pl.BlockSpec((512, 384), lambda i: (0, 0)),
            pl.BlockSpec(index.shape, lambda i: (0, 0)),
        ],
        out_specs=pl.BlockSpec((3, elems, 512), lambda i: (0, 0, 0)),
        out_shape=jax.ShapeDtypeStruct((3, elems, 512), F32),
        scratch_shapes=[pltpu.VMEM((6 * peers, capacity), BF16)]
        + [pltpu.VMEM((3, elems, 384), F32)] * 3
        + [pltpu.SemaphoreType.DMA((6,))] * 2,
        compiler_params=pltpu.CompilerParams(
            dimension_semantics=("arbitrary",), collective_id=1, has_side_effects=True
        ),
        name="finish",
    )(answers, owner, slot, jnp.asarray(face_selector(), BF16), index)


def local(velocity, depart, owner_rank, owner_element_index, neighbours):
    outer, inner = lax.axis_size("gx"), lax.axis_size("gy")
    peers = outer * inner
    elems = velocity.shape[1]
    points = depart.shape[1]
    capacity = 2 * points // peers
    owner = owner_rank.reshape(1, points)
    table = velocity.reshape(3, elems, 64, 8).transpose(0, 2, 1, 3).reshape(192, elems * 8)
    elem = owner_element_index.reshape(1, points)
    answers, slot = exchange(owner, depart, elem, table, outer, inner, capacity)
    device_id = lax.axis_index("gx") * inner + lax.axis_index("gy")
    index = jnp.where(neighbours >= 0, neighbours - (device_id - 1) * elems, -1)
    return finish(answers, owner, slot, index.reshape(6 * elems, 1), elems, outer, inner)


def solution(mesh):
    placed = (
        P(None, ("gx", "gy"), None),
        P(None, ("gx", "gy")),
        P(("gx", "gy"), None),
        P(("gx", "gy")),
        P(None, ("gx", "gy")),
    )
    return jax.shard_map(
        local, mesh=mesh, in_specs=placed, out_specs=P(None, ("gx", "gy"), None), check_vma=False
    )
```
